32 devices in a mesh: row: 8 (over y, x, core), ctx: 4 (over z).
Axes of the slice: x: 2, y: 2, z: 4, core: 2. Of those that a mesh axis runs over, the one named last changes fastest.
Arguments:
- queries: bfloat16 [5, 4096, 128], P(None, ('row', 'ctx')), may hold values from -100 to 100
- keys: bfloat16 [4096, 128], P('ctx'), may hold values from -6 to 6
- doc_ids: int32 [64], replicated, may hold values from 0 to 3, never falling along the last dimension, each value on 1 to 48 neighbouring positions
- gate_query: bfloat16 [5, 128, 128], replicated, may hold values from -0.5 to 0.5
- gate_key: bfloat16 [384, 128], replicated, may hold values from -0.3125 to 0.3125
Outputs:
- block_map: float32 [5, 64, 64], P(None, ('row', 'ctx'))
- grad_query: float32 [5, 128, 128], replicated
- grad_key: float32 [384, 128], replicated
The draws below stay inside these ranges and needn't reach their ends.
Inputs may be any that keep to these rules, and one draw needn't show every extreme that they name: `doc_ids`: block document ids never fall along the sequence; each document spans 1 to 48 blocks and one spans exactly 48.
All inputs are finite; a program needn't handle non-finite values.
Results may differ from the reference program's by a relative error of at most 0.0003.
Values may be sent and summed in bfloat16 or wider, within the bound.
A program may use at most 64 MiB of HBM per device.

```python
import math
import jax
import jax.numpy as jnp
import numpy as np
from jax import lax

H = 5
HD = 128
DG = 128
BLK = 64
DOCS = 4
TOKENS = 4096
KB = 64
MOST = 48


def make_pair(key):
    base_key = jax.random.fold_in(key, 7)
    key_one, key_two = jax.random.split(base_key, 2)
    key_rows = jnp.clip(jax.random.normal(key_one, (TOKENS, HD), jnp.float32), -6.0, 6.0)
    query_rows = jnp.clip(jax.random.normal(key_two, (H, TOKENS, HD), jnp.float32), -6.0, 6.0)
    return (query_rows, key_rows)


def draw_queries(key, part):
    return make_pair(key)[0].astype(jnp.bfloat16)


def draw_keys(key, part):
    return make_pair(key)[1].astype(jnp.bfloat16)


def split_up(number_of, total, most, lean):
    portions = [(1 << 20) // math.isqrt(grade ** lean) + 1 for grade in range(2, number_of + 1)]
    spare, given = total - most - (number_of - 1), [1] * (number_of - 1)
    while spare > 0:
        free = [i for i in range(number_of - 1) if given[i] < most]
        pool, budget = sum([portions[i] for i in free]), spare
        for i in free:
            more = min(most - given[i], max(1, budget * portions[i] // pool), spare)
            given[i] = given[i] + more
            spare = spare - more
    return np.array([most] + given)


def ragged_sizes(key, amount, total, most, skew):
    if amount == 2:
        one = jax.random.randint(key, (), max(1, total - most), min(most, total - 1) + 1)
        return jnp.stack([one, total - one])
    sizes = jnp.asarray(split_up(amount, total, most, skew), jnp.int32)
    couples = (amount - 1) // 2
    giver, taker = sizes[1:1 + 2 * couples:2], sizes[2:2 + 2 * couples:2]
    room = jnp.minimum(giver - 1, most - taker)
    shifted = jax.random.randint(jax.random.fold_in(key, 1), (couples,), 0, 1 << 20) % (room + 1)
    sizes = sizes.at[1:1 + 2 * couples:2].set(giver - shifted).at[2:2 + 2 * couples:2].set(taker + shifted)
    return sizes[jax.random.permutation(jax.random.fold_in(key, 2), amount)]


def noise(key, dims, scale, reach, kind=jnp.bfloat16):
    return jnp.clip(scale * jax.random.normal(key, dims, jnp.float32), -reach, reach).astype(kind)


def setup_inputs(seed: int = 0) -> dict:
    splits = jax.random.split(jax.random.key(seed), 6)
    queries = draw_queries(jax.random.fold_in(splits[5], 71), 0)
    keys = draw_keys(jax.random.fold_in(splits[5], 71), 0)
    doc_ids = jnp.searchsorted(jnp.cumsum(ragged_sizes(splits[2], DOCS, KB, MOST, 2)), jnp.arange(KB), side="right").astype(jnp.int32)
    gate_query = noise(splits[3], (H, HD, DG), HD ** -0.5, 0.5)
    gate_key = noise(splits[4], (3 * HD, DG), (3 * HD) ** -0.5, 0.3125)
    return {"queries": queries, "keys": keys, "doc_ids": doc_ids, "gate_query": gate_query, "gate_key": gate_key}


NEG_FILL = -1e+30

def reference(queries, keys, doc_ids, gate_query, gate_key):
    score_scale = 1.0 / math.sqrt(HD)
    key_doc = jnp.repeat(doc_ids, BLK)
    key_pos = jnp.arange(TOKENS, dtype=jnp.int32)
    keys_wide = keys.astype(jnp.float32)

    def one_block(block_index):
        query_rows = lax.dynamic_slice_in_dim(queries, (block_index * BLK).astype(jnp.int32), BLK, 1).astype(jnp.float32)
        scores = jnp.einsum('hrd,kd->hrk', query_rows, keys_wide, precision=lax.Precision.HIGHEST) * score_scale
        query_pos = block_index * BLK + jnp.arange(BLK, dtype=jnp.int32)
        query_doc = doc_ids[block_index]
        allowed = (key_pos[None, :] <= query_pos[:, None]) & (key_doc[None, :] == query_doc)
        masked = jnp.where(allowed[None], scores, NEG_FILL)
        row_top = lax.optimization_barrier(jnp.max(masked, axis=2))
        row_total = lax.optimization_barrier(jnp.sum(jnp.where(allowed[None], jnp.exp(masked - row_top[:, :, None]), 0.0), axis=2))
        log_total = row_top + jnp.log(row_total)
        block_peaks = lax.optimization_barrier(jnp.max(masked.reshape(H, BLK, KB, BLK), axis=3))
        return lax.optimization_barrier(jnp.max(jnp.exp(block_peaks - log_total[:, :, None]), axis=1))
    block_map = jnp.transpose(lax.map(one_block, jnp.arange(KB, dtype=jnp.int32)), (1, 0, 2))
    query_pool = lax.optimization_barrier(jnp.mean(queries.astype(jnp.float32).reshape(H, KB, BLK, HD), axis=2))
    grouped = keys_wide.reshape(KB, BLK, HD)
    key_pool = jnp.concatenate([lax.optimization_barrier(jnp.max(grouped, axis=1)), lax.optimization_barrier(jnp.min(grouped, axis=1)), lax.optimization_barrier(jnp.mean(grouped, axis=1))], axis=1)
    query_gate = jnp.einsum('hbd,hde->hbe', query_pool, gate_query.astype(jnp.float32), precision=lax.Precision.HIGHEST)
    key_gate = jnp.dot(key_pool, gate_key.astype(jnp.float32), precision=lax.Precision.HIGHEST)
    gate_logits = jnp.einsum('hbe,ke->hbk', query_gate, key_gate, precision=lax.Precision.HIGHEST)
    blocks = jnp.arange(KB, dtype=jnp.int32)
    block_allowed = (blocks[None, :] <= blocks[:, None]) & (doc_ids[None, :] == doc_ids[:, None])
    gate_exp = jnp.where(block_allowed[None], jnp.exp(gate_logits), 0.0)
    gate_prob = gate_exp / lax.optimization_barrier(jnp.sum(gate_exp, axis=2, keepdims=True))
    target = block_map / lax.optimization_barrier(jnp.sum(block_map, axis=2, keepdims=True))
    diff = gate_prob - target
    query_back = jnp.einsum('hbk,ke->hbe', diff, key_gate, precision=lax.Precision.HIGHEST)
    grad_query = jnp.einsum('hbd,hbe->hde', query_pool, query_back, precision=lax.Precision.HIGHEST)
    key_back = jnp.einsum('hbk,hbe->ke', diff, query_gate, precision=lax.Precision.HIGHEST)
    grad_key = jnp.dot(key_pool.T, key_back, precision=lax.Precision.HIGHEST)
    return (block_map, grad_query, grad_key)
```

```python
import functools
import math

import jax
import jax.numpy as jnp
from jax import lax
from jax.experimental import pallas as pl
from jax.experimental.pallas import tpu as pltpu
from jax.sharding import PartitionSpec as P

BLK = 64
NEG = -1e30
PIECE = 16
GROUP = 4
MOST = (3, 4)
MESH = pl.DeviceIdType.MESH
VMEM_LIMIT = 32 * 1024 * 1024
HI = lax.Precision.HIGHEST


def fdot(a, b, dims):
    return lax.dot_general(a, b, (dims, ((), ())), precision=HI, preferred_element_type=jnp.float32)


def gate(a, w):
    m = a.shape[0]
    hi = a.astype(jnp.bfloat16)
    rest = a - hi.astype(jnp.float32)
    mid = rest.astype(jnp.bfloat16)
    low = (rest - mid.astype(jnp.float32)).astype(jnp.bfloat16)
    p = jnp.dot(
        jnp.concatenate([hi, mid, low], axis=0), w, preferred_element_type=jnp.float32
    )
    return p[:m] + (p[m:2 * m] + p[2 * m:])


def kernel(
    R, C, q_hbm, k_hbm, doc_hbm, gq_hbm, gk_hbm,
    bm_ref, qp_ref, qg_ref, both_ref, pooled_ref, diff_ref,
    q_ref, gq_ref, gk_ref, doc_ref, kbuf, q_t, peak, bsum, kpool, pieces, diff_own, diff_all,
    local, keysent, rsem, ps1, ps2, ps3, pctx, prow, ds1, dctx,
):
    H, rows, D = q_ref.shape
    shard = R * rows
    nb = rows // BLK
    n = R * C
    TB = n * nb
    most = TB * MOST[0] // MOST[1]
    r = lax.axis_index("row")
    c = lax.axis_index("ctx")
    me = r * C + c
    half = R // 2
    scale = 1.0 / math.sqrt(D)
    used = H * nb
    cut = rows // 2

    def ctx_peer(d):
        return lax.rem(c + d, C)

    def flip(rr, e):
        bit = 2
        while e:
            if e % 2:
                rr = rr + bit - 2 * bit * lax.rem(rr // bit, 2)
            e, bit = e // 2, bit * 2
        return rr

    def row_peer(e):
        return flip(r, e)

    partner = r + 1 - 2 * lax.rem(r, 2)

    def other_row(e):
        return flip(partner, e)

    def others(i):
        return jnp.where(i >= c, i + 1, i)

    def far_first(i):
        down = C - 1 - i
        return jnp.where(2 * c < C, jnp.where(down <= c, down - 1, down), others(i))

    barrier = pltpu.get_barrier_semaphore()
    for d in range(1, C):
        pl.semaphore_signal(barrier, inc=1, device_id=(r, ctx_peer(d)), device_id_type=MESH)
    for e in range(1, half):
        pl.semaphore_signal(barrier, inc=1, device_id=(row_peer(e), c), device_id_type=MESH)
    pl.semaphore_signal(barrier, inc=1, device_id=(partner, c), device_id_type=MESH)

    def chunk(num):
        return pl.ds(pl.multiple_of(num * rows, rows), rows)

    def piece(num, x):
        return pl.ds(pl.multiple_of(num * rows + x * cut, cut), cut)

    def part(rr):
        return pl.ds(pl.multiple_of(rr * PIECE, PIECE), used)

    loads = [
        pltpu.make_async_copy(q_hbm, q_ref, local.at[0]),
        pltpu.make_async_copy(
            k_hbm, kbuf.at[pl.ds(pl.multiple_of(c * shard, shard), shard)], local.at[1]
        ),
        pltpu.make_async_copy(doc_hbm, doc_ref, local.at[2]),
        pltpu.make_async_copy(gq_hbm, gq_ref, local.at[3]),
        pltpu.make_async_copy(gk_hbm, gk_ref, local.at[4]),
    ]
    for load in loads:
        load.start()
    peak[...] = jnp.full_like(peak, NEG)
    bsum[...] = jnp.zeros_like(bsum)
    loads[0].wait()
    for h in range(H):
        qf = q_ref[h].astype(jnp.float32)
        q_t[:, h * rows:(h + 1) * rows] = qf.T.astype(jnp.bfloat16)
        for j in range(nb):
            pieces[c, pl.ds(r * PIECE + h * nb + j, 1), :] = jnp.mean(
                qf[j * BLK:(j + 1) * BLK], axis=0, keepdims=True
            )
    pl.semaphore_wait(barrier, C - 1 + half)

    def copy_ctx(cc):
        return pltpu.make_async_remote_copy(
            src_ref=k_hbm.at[pl.ds(pl.multiple_of(r * rows, rows), rows)],
            dst_ref=kbuf.at[chunk(c * R + r)],
            send_sem=keysent.at[0], recv_sem=rsem.at[c * R + r, 0],
            device_id=(r, cc), device_id_type=MESH,
        )

    def copy_whole(num, to):
        return pltpu.make_async_remote_copy(
            src_ref=kbuf.at[chunk(num)], dst_ref=kbuf.at[chunk(num)],
            send_sem=keysent.at[0], recv_sem=rsem.at[num, 0],
            device_id=(to, c), device_id_type=MESH,
        )

    def copy_half(num, x, to):
        return pltpu.make_async_remote_copy(
            src_ref=kbuf.at[piece(num, x)], dst_ref=kbuf.at[piece(num, x)],
            send_sem=keysent.at[0], recv_sem=rsem.at[num, x],
            device_id=(to, c), device_id_type=MESH,
        )

    def arrived(num):
        at = kbuf.at[chunk(num)]
        pltpu.make_async_copy(at, at, rsem.at[num, 0]).wait()

    def half_arrived(num, x):
        at = kbuf.at[piece(num, x)]
        pltpu.make_async_copy(at, at, rsem.at[num, x]).wait()

    def piece1(d):
        return pltpu.make_async_remote_copy(
            src_ref=pieces.at[c, part(r)], dst_ref=pieces.at[c, part(r)],
            send_sem=ps1.at[d], recv_sem=pctx.at[c],
            device_id=(r, ctx_peer(d)), device_id_type=MESH,
        )

    def piece2(e):
        return pltpu.make_async_remote_copy(
            src_ref=pieces.at[:, part(r)], dst_ref=pieces.at[:, part(r)],
            send_sem=ps2.at[e], recv_sem=prow.at[r],
            device_id=(row_peer(e), c), device_id_type=MESH,
        )

    def piece3(e):
        rr = row_peer(e)
        return pltpu.make_async_remote_copy(
            src_ref=pieces.at[:, part(rr)], dst_ref=pieces.at[:, part(rr)],
            send_sem=ps3.at[e], recv_sem=prow.at[rr],
            device_id=(partner, c), device_id_type=MESH,
        )

    def row_arrived(rr):
        pltpu.make_async_copy(
            pieces.at[:, part(rr)], pieces.at[:, part(rr)], prow.at[rr]
        ).wait()

    @pl.loop(0, C - 1)
    def _(i):
        copy_ctx(far_first(i)).start()

    for d in range(1, C):
        piece1(d).start()

    loads[2].wait()
    a0 = me * nb
    lane = lax.broadcasted_iota(jnp.int32, (1, 2 * rows), 1)
    qdoc = jnp.zeros((1, 2 * rows), jnp.int32)
    for j in range(nb):
        qdoc = jnp.where(lax.rem(lane, rows) // BLK == j, doc_ref[a0 + j], qdoc)

    def score(nums, masked):
        keys = jnp.concatenate([kbuf[chunk(num), :] for num in nums], axis=0)
        for h in range(0, H, 2):
            width = min(2, H - h) * rows
            cols = slice(h * rows, h * rows + width)
            s = jnp.dot(keys, q_t[:, cols], preferred_element_type=jnp.float32)
            if masked:
                ki = lax.broadcasted_iota(jnp.int32, s.shape, 0)
                qi = lax.rem(lax.broadcasted_iota(jnp.int32, s.shape, 1), rows)
                s = jnp.where(ki - qi <= (me - nums[0]) * rows, s, NEG)
            for m, num in enumerate(nums):
                for j in range(nb):
                    b = num * nb + j
                    at = (m * nb + j) * BLK
                    t = s[at:at + BLK]
                    top = jnp.max(t, axis=0, keepdims=True)
                    total = jnp.sum(
                        jnp.exp2((t - top) * (scale * math.log2(math.e))), axis=0, keepdims=True
                    )
                    top = jnp.where(qdoc[:, :width] == doc_ref[b], top * scale, NEG)
                    for k in range(width // rows):
                        peak[h + k, pl.ds(b, 1), :] = top[:, k * rows:(k + 1) * rows]
                        bsum[h + k, pl.ds(b, 1), :] = total[:, k * rows:(k + 1) * rows]

    def pool(num):
        wide = kbuf[chunk(num), :].astype(jnp.float32)
        for j in range(nb):
            t = wide[j * BLK:(j + 1) * BLK]
            for i, how in enumerate((jnp.max, jnp.min, jnp.mean)):
                kpool[i, pl.ds(num * nb + j, 1), :] = how(t, axis=0, keepdims=True)

    def near(num):
        return (num + 1) * nb - 1 + most > a0

    def process(nums):
        for num in nums:
            pool(num)
        whole = (nums[0] < me) & near(nums[0])
        for num in nums[1:]:
            whole = whole & (num < me) & near(num)

        @pl.when(whole)
        def _():
            for i in range(0, len(nums), 2):
                score(nums[i:i + 2], False)

        @pl.when(jnp.logical_not(whole))
        def _():
            for num in nums:
                @pl.when((num <= me) & near(num))
                def _():
                    score([num], True)

    loads[1].wait()

    @pl.loop(0, half)
    def _(g):
        process([c * R + 2 * g, c * R + 2 * g + 1])

    @pl.loop(0, C - 1)
    def _(i):
        num = others(i) * R + r
        arrived(num)
        copy_half(num, 0, row_peer(1)).start()
        copy_half(num, 1, row_peer(2)).start()
        copy_half(num, 1, row_peer(1)).start()
        copy_half(num, 0, row_peer(2)).start()
        for e in range(4, half):
            copy_whole(num, row_peer(e)).start()
        copy_whole(num, partner).start()

    @pl.loop(0, C - 1)
    def _(i):
        base = others(i) * R
        half_arrived(base + row_peer(1), 0)
        copy_half(base + row_peer(1), 0, row_peer(2)).start()
        half_arrived(base + row_peer(2), 1)
        copy_half(base + row_peer(2), 1, row_peer(1)).start()

    for d in range(1, C):
        cc = ctx_peer(d)
        pltpu.make_async_copy(pieces.at[cc, part(r)], pieces.at[cc, part(r)], pctx.at[cc]).wait()
    for e in range(1, half):
        piece2(e).start()
    piece3(0).start()

    @pl.loop(0, C - 1)
    def _(i):
        base = others(i) * R
        half_arrived(base + row_peer(1), 1)
        copy_whole(base + row_peer(1), partner).start()
        half_arrived(base + row_peer(2), 0)
        copy_whole(base + row_peer(2), partner).start()

    @pl.loop(0, C - 1)
    def _(i):
        base = others(i) * R
        arrived(base + partner)
        process([base + r, base + partner, base + row_peer(1), base + row_peer(2)])

    @pl.loop(0, C - 1)
    def _(i):
        num = others(i) * R + row_peer(3)
        half_arrived(num, 0)
        half_arrived(num, 1)
        copy_whole(num, partner).start()
        for e in range(4, half):
            arrived(others(i) * R + row_peer(e))
            copy_whole(others(i) * R + row_peer(e), partner).start()

    @pl.loop(0, C - 1)
    def _(i):
        base = others(i) * R
        arrived(base + other_row(1))
        arrived(base + other_row(2))
        process([base + row_peer(3), base + other_row(1), base + other_row(2)])

    for e in range(1, half):
        row_arrived(row_peer(e))
        piece3(e).start()

    @pl.loop(0, C - 1)
    def _(i):
        base = others(i) * R
        arrived(base + other_row(3))
        process([base + other_row(3)])
        for e in range(4, half):
            arrived(base + other_row(e))
            process([base + row_peer(e), base + other_row(e)])

    loads[3].wait()
    loads[4].wait()
    pooled = jnp.concatenate([kpool[i] for i in range(3)], axis=1)
    key_gate = gate(pooled, gk_ref[...])
    row16 = lax.broadcasted_iota(jnp.int32, (PIECE, 1), 0)
    own = jnp.where(row16 < used, pieces[c, pl.ds(pl.multiple_of(r * PIECE, PIECE), PIECE), :], 0.0)
    qg = jnp.zeros((PIECE, D), jnp.float32)
    for h in range(H):
        qg = jnp.where(row16 // nb == h, gate(own, gq_ref[h]), qg)
    logits = fdot(qg, key_gate, ((1,), (1,)))

    maps = jnp.full((PIECE, TB), NEG, jnp.float32)
    for h in range(H):
        pk = peak[h]
        top = jnp.max(pk, axis=0, keepdims=True)
        total = jnp.sum(bsum[h] * jnp.exp(pk - top), axis=0, keepdims=True)
        chance = (pk - (top + jnp.log(total))).T
        for j in range(nb):
            best = jnp.max(chance[j * BLK:(j + 1) * BLK], axis=0, keepdims=True)
            maps = jnp.where(row16 == h * nb + j, best, maps)
    allowed = maps > 0.01 * NEG
    block_map = jnp.where(allowed, jnp.exp(maps), 0.0)
    live = row16 < used
    gate_exp = jnp.where(allowed, jnp.exp(logits), 0.0)
    gate_sum = jnp.where(live, jnp.sum(gate_exp, axis=1, keepdims=True), 1.0)
    map_sum = jnp.where(live, jnp.sum(block_map, axis=1, keepdims=True), 1.0)
    diff = gate_exp / gate_sum - block_map / map_sum
    for h in range(H):
        for j in range(nb):
            diff_own[h:h + 1, j * TB:(j + 1) * TB] = diff[h * nb + j:h * nb + j + 1, :]

    def send(d, e):
        to_row, to_ctx = r + e, c + d
        to_row = jnp.where(to_row >= R, to_row - R, to_row)
        to_ctx = jnp.where(to_ctx >= C, to_ctx - C, to_ctx)
        return pltpu.make_async_remote_copy(
            src_ref=diff_own, dst_ref=diff_all.at[c * R + r],
            send_sem=ds1.at[0], recv_sem=dctx.at[0],
            device_id=(to_row, to_ctx), device_id_type=MESH,
        )

    for e in range(R - 1, -1, -1):
        for d in range(C - 1, -1, -1):
            if d or e:
                send(d, e).start()
    diff_all[c * R + r] = diff_own[...]
    for h in range(H):
        for j in range(nb):
            bm_ref[h, j:j + 1, :] = block_map[h * nb + j:h * nb + j + 1, :]

    for e in range(half):
        row_arrived(other_row(e))

    def gathered(j):
        return jnp.concatenate(
            [pieces[i, pl.ds(j, R, stride=PIECE), :] for i in range(C)], axis=0
        )

    for h in range(H):
        qp = jnp.concatenate([gathered(h * nb + j) for j in range(nb)], axis=0)
        qp_ref[h] = qp
        qg_ref[h] = gate(qp, gq_ref[h])

    for j in range(nb):
        both_ref[j * TB:(j + 1) * TB] = key_gate
    pooled_ref[...] = pooled
    rest = diff_all.at[pl.ds(0, n - 1)]
    pltpu.make_async_copy(rest, rest, dctx.at[0]).wait()
    diff_ref[...] = diff_all[...]
    pltpu.make_async_copy(rest, rest, ds1.at[0]).wait()
    sent = kbuf.at[pl.ds(0, (C - 1) * shard)]
    pltpu.make_async_copy(sent, sent, keysent.at[0]).wait()
    for d in range(1, C):
        piece1(d).wait_send()
    for e in range(half):
        piece3(e).wait_send()
        if e > 0:
            piece2(e).wait_send()


def finish(map_ref, qp_ref, qg_ref, both_ref, pooled_ref, diff_ref, bm_ref, dq_ref, dk_ref):
    H, nb, TB = map_ref.shape
    bm_ref[...] = map_ref[...]
    both = both_ref[...]
    wide_lane = lax.broadcasted_iota(jnp.int32, (1, nb * TB), 1)
    key_back = jnp.zeros(both.shape, jnp.float32)
    for h in range(H):
        mixed = diff_ref[:, h, :]
        diff = jnp.concatenate(
            [jnp.where(wide_lane // TB == j, mixed, 0.0) for j in range(nb)], axis=0
        )
        back = fdot(diff, both, ((1,), (0,)))
        dq_ref[h] = fdot(qp_ref[h], back, ((0,), (0,)))
        key_back = key_back + fdot(diff, qg_ref[h], ((0,), (0,)))
    folded = key_back[:TB]
    for j in range(1, nb):
        folded = folded + key_back[j * TB:(j + 1) * TB]
    dk_ref[...] = fdot(pooled_ref[...], folded, ((0,), (0,)))


def shards(R, C, queries, keys, doc_ids, gate_query, gate_key):
    H, rows, D = queries.shape
    n = R * C
    nb = rows // BLK
    TB = doc_ids.shape[0]
    half = R // 2
    vm = pl.BlockSpec(memory_space=pltpu.VMEM)
    hbm = pl.BlockSpec(memory_space=pltpu.HBM)
    dma = pltpu.SemaphoreType.DMA
    given = [
        pltpu.with_memory_space_constraint(x, pltpu.HBM)
        for x in (queries, keys, doc_ids, gate_query, gate_key)
    ]
    parts = pl.pallas_call(
        functools.partial(kernel, R, C),
        out_shape=(
            jax.ShapeDtypeStruct((H, nb, TB), jnp.float32),
            jax.ShapeDtypeStruct((H, nb * n, D), jnp.float32),
            jax.ShapeDtypeStruct((H, nb * n, D), jnp.float32),
            jax.ShapeDtypeStruct((nb * TB, D), jnp.float32),
            jax.ShapeDtypeStruct((TB, 3 * D), jnp.float32),
            jax.ShapeDtypeStruct((n, H, nb * TB), jnp.float32),
        ),
        in_specs=[hbm] * 5,
        out_specs=(vm,) * 6,
        scratch_shapes=[
            pltpu.VMEM(queries.shape, queries.dtype),
            pltpu.VMEM(gate_query.shape, gate_query.dtype),
            pltpu.VMEM(gate_key.shape, gate_key.dtype),
            pltpu.SMEM(doc_ids.shape, doc_ids.dtype),
            pltpu.VMEM((C * keys.shape[0], D), jnp.bfloat16),
            pltpu.VMEM((D, H * rows), jnp.bfloat16),
            pltpu.VMEM((H, TB, rows), jnp.float32),
            pltpu.VMEM((H, TB, rows), jnp.float32),
            pltpu.VMEM((3, TB, D), jnp.float32),
            pltpu.VMEM((C, R * PIECE, D), jnp.float32),
            pltpu.VMEM((H, nb * TB), jnp.float32),
            pltpu.VMEM((n, H, nb * TB), jnp.float32),
            dma((5,)), dma((1,)), dma((n, 2)),
            dma((C,)), dma((half,)), dma((half,)), dma((C,)), dma((R,)), dma((1,)), dma((1,)),
        ],
        compiler_params=pltpu.CompilerParams(
            collective_id=0, has_side_effects=True, vmem_limit_bytes=VMEM_LIMIT
        ),
    )(*given)
    return pl.pallas_call(
        finish,
        out_shape=(
            jax.ShapeDtypeStruct((H, nb, TB), jnp.float32),
            jax.ShapeDtypeStruct(gate_query.shape, jnp.float32),
            jax.ShapeDtypeStruct(gate_key.shape, jnp.float32),
        ),
        in_specs=[vm] * 6,
        out_specs=(vm,) * 3,
        compiler_params=pltpu.CompilerParams(vmem_limit_bytes=VMEM_LIMIT),
    )(*parts)


def solution(mesh):
    R, C = mesh.shape["row"], mesh.shape["ctx"]
    in_specs = (P(None, ("row", "ctx"), None), P("ctx", None), P(), P(), P())
    out_specs = (P(None, ("row", "ctx"), None), P(), P())
    return jax.shard_map(
        functools.partial(shards, R, C), mesh=mesh, in_specs=in_specs, out_specs=out_specs,
        check_vma=False,
    )
```

```python
import functools
import math

import jax
import jax.numpy as jnp
from jax import lax
from jax.experimental import pallas as pl
from jax.experimental.pallas import tpu as pltpu
from jax.sharding import PartitionSpec as P

BLK = 64
NEG = -1e30
PIECE = 16
GROUP = 4
MOST = (3, 4)
MESH = pl.DeviceIdType.MESH
VMEM_LIMIT = 32 * 1024 * 1024
HI = lax.Precision.HIGHEST


def fdot(a, b, dims):
    return lax.dot_general(a, b, (dims, ((), ())), precision=HI, preferred_element_type=jnp.float32)


def gate(a, w):
    m = a.shape[0]
    hi = a.astype(jnp.bfloat16)
    rest = a - hi.astype(jnp.float32)
    mid = rest.astype(jnp.bfloat16)
    low = (rest - mid.astype(jnp.float32)).astype(jnp.bfloat16)
    p = jnp.dot(
        jnp.concatenate([hi, mid, low], axis=0), w, preferred_element_type=jnp.float32
    )
    return p[:m] + (p[m:2 * m] + p[2 * m:])


def kernel(
    R, C, q_hbm, k_hbm, doc_hbm, gq_hbm, gk_hbm,
    bm_ref, qp_ref, qg_ref, both_ref, pooled_ref, diff_ref,
    q_ref, gq_ref, gk_ref, doc_ref, kbuf, q_t, peak, bsum, kpool, pieces, diff_own, diff_all,
    local, keysent, rsem, psem, ds1, dctx,
):
    H, rows, D = q_ref.shape
    shard = R * rows
    nb = rows // BLK
    n = R * C
    TB = n * nb
    most = TB * MOST[0] // MOST[1]
    r = lax.axis_index("row")
    c = lax.axis_index("ctx")
    me = r * C + c
    half = R // 2
    scale = 1.0 / math.sqrt(D)
    used = H * nb
    cut = rows // 2

    def ctx_peer(d):
        return lax.rem(c + d, C)

    def flip(rr, e):
        bit = 2
        while e:
            if e % 2:
                rr = rr + bit - 2 * bit * lax.rem(rr // bit, 2)
            e, bit = e // 2, bit * 2
        return rr

    def row_peer(e):
        return flip(r, e)

    partner = r + 1 - 2 * lax.rem(r, 2)

    def other_row(e):
        return flip(partner, e)

    def others(i):
        return jnp.where(i >= c, i + 1, i)

    def far_first(i):
        down = C - 1 - i
        return jnp.where(2 * c < C, jnp.where(down <= c, down - 1, down), others(i))

    barrier = pltpu.get_barrier_semaphore()
    for d in range(1, C):
        pl.semaphore_signal(barrier, inc=1, device_id=(r, ctx_peer(d)), device_id_type=MESH)
    for e in range(1, half):
        pl.semaphore_signal(barrier, inc=1, device_id=(row_peer(e), c), device_id_type=MESH)
    pl.semaphore_signal(barrier, inc=1, device_id=(partner, c), device_id_type=MESH)

    def chunk(num):
        return pl.ds(pl.multiple_of(num * rows, rows), rows)

    def piece(num, x):
        return pl.ds(pl.multiple_of(num * rows + x * cut, cut), cut)

    def part(rr):
        return pl.ds(pl.multiple_of(rr * PIECE, PIECE), used)

    loads = [
        pltpu.make_async_copy(q_hbm, q_ref, local.at[0]),
        pltpu.make_async_copy(
            k_hbm, kbuf.at[pl.ds(pl.multiple_of(c * shard, shard), shard)], local.at[1]
        ),
        pltpu.make_async_copy(doc_hbm, doc_ref, local.at[2]),
        pltpu.make_async_copy(gq_hbm, gq_ref, local.at[3]),
        pltpu.make_async_copy(gk_hbm, gk_ref, local.at[4]),
    ]
    for load in loads:
        load.start()
    pl.semaphore_wait(barrier, C - 1 + half)

    def place(at, cc):
        return jnp.where(at < cc, at, at - 1)

    def copy_ctx(cc):
        return pltpu.make_async_remote_copy(
            src_ref=k_hbm.at[pl.ds(pl.multiple_of(r * rows, rows), rows)],
            dst_ref=kbuf.at[chunk(c * R + r)],
            send_sem=keysent.at[0], recv_sem=rsem.at[place(c, cc), 0],
            device_id=(r, cc), device_id_type=MESH,
        )

    def copy_in(at, p, kind, to):
        return pltpu.make_async_remote_copy(
            src_ref=kbuf.at[at], dst_ref=kbuf.at[at],
            send_sem=keysent.at[0], recv_sem=rsem.at[p, kind],
            device_id=(to, c), device_id_type=MESH,
        )

    def arrived(p, kind, size):
        at = kbuf.at[pl.ds(0, size)]
        pltpu.make_async_copy(at, at, rsem.at[p, kind]).wait()

    def copy_piece(at, kind, device):
        return pltpu.make_async_remote_copy(
            src_ref=pieces.at[at], dst_ref=pieces.at[at],
            send_sem=psem.at[3], recv_sem=psem.at[kind],
            device_id=device, device_id_type=MESH,
        )

    def pieces_arrived(kind, count):
        at = kbuf.at[pl.ds(0, 2 * used * count)]
        pltpu.make_async_copy(at, at, psem.at[kind]).wait()

    @pl.loop(0, C - 1)
    def _(i):
        copy_ctx(far_first(i)).start()

    peak[...] = jnp.full_like(peak, NEG)
    bsum[...] = jnp.zeros_like(bsum)
    loads[0].wait()
    for h in range(H):
        qf = q_ref[h].astype(jnp.float32)
        q_t[:, h * rows:(h + 1) * rows] = qf.T.astype(jnp.bfloat16)
        for j in range(nb):
            pieces[c, pl.ds(r * PIECE + h * nb + j, 1), :] = jnp.mean(
                qf[j * BLK:(j + 1) * BLK], axis=0, keepdims=True
            )

    loads[2].wait()
    a0 = me * nb
    lane = lax.broadcasted_iota(jnp.int32, (1, 2 * rows), 1)
    qdoc = jnp.zeros((1, 2 * rows), jnp.int32)
    for j in range(nb):
        qdoc = jnp.where(lax.rem(lane, rows) // BLK == j, doc_ref[a0 + j], qdoc)

    def score(nums, masked):
        keys = jnp.concatenate([kbuf[chunk(num), :] for num in nums], axis=0)
        for h in range(0, H, 2):
            width = min(2, H - h) * rows
            cols = slice(h * rows, h * rows + width)
            s = jnp.dot(keys, q_t[:, cols], preferred_element_type=jnp.float32)
            if masked:
                ki = lax.broadcasted_iota(jnp.int32, s.shape, 0)
                qi = lax.rem(lax.broadcasted_iota(jnp.int32, s.shape, 1), rows)
                s = jnp.where(ki - qi <= (me - nums[0]) * rows, s, NEG)
            for m, num in enumerate(nums):
                for j in range(nb):
                    b = num * nb + j
                    at = (m * nb + j) * BLK
                    t = s[at:at + BLK]
                    top = jnp.max(t, axis=0, keepdims=True)
                    total = jnp.sum(
                        jnp.exp2((t - top) * (scale * math.log2(math.e))), axis=0, keepdims=True
                    )
                    top = jnp.where(qdoc[:, :width] == doc_ref[b], top * scale, NEG)
                    for k in range(width // rows):
                        peak[h + k, pl.ds(b, 1), :] = top[:, k * rows:(k + 1) * rows]
                        bsum[h + k, pl.ds(b, 1), :] = total[:, k * rows:(k + 1) * rows]

    def pool(num):
        wide = kbuf[chunk(num), :].astype(jnp.float32)
        for j in range(nb):
            t = wide[j * BLK:(j + 1) * BLK]
            for i, how in enumerate((jnp.max, jnp.min, jnp.mean)):
                kpool[i, pl.ds(num * nb + j, 1), :] = how(t, axis=0, keepdims=True)

    def near(num):
        return (num + 1) * nb - 1 + most > a0

    def process(nums):
        whole = (nums[0] < me) & near(nums[0])
        for num in nums[1:]:
            whole = whole & (num < me) & near(num)

        @pl.when(whole)
        def _():
            for i in range(0, len(nums), 2):
                score(nums[i:i + 2], False)

        @pl.when(jnp.logical_not(whole))
        def _():
            for num in nums:
                @pl.when((num <= me) & near(num))
                def _():
                    score([num], True)

    loads[1].wait()

    @pl.loop(0, half)
    def _(g):
        pool(c * R + 2 * g)
        pool(c * R + 2 * g + 1)
        process([c * R + 2 * g, c * R + 2 * g + 1])

    loads[3].wait()
    loads[4].wait()
    row16 = lax.broadcasted_iota(jnp.int32, (PIECE, 1), 0)
    own = jnp.where(row16 < used, pieces[c, pl.ds(pl.multiple_of(r * PIECE, PIECE), PIECE), :], 0.0)
    qg = jnp.zeros((PIECE, D), jnp.float32)
    for h in range(H):
        qg = jnp.where(row16 // nb == h, gate(own, gq_ref[h]), qg)

    one, two, three = (row_peer(e) for e in (1, 2, 3))

    @pl.loop(0, C - 1)
    def _(i):
        num = others(i) * R + r
        arrived(i, 0, rows)
        copy_in(piece(num, 0), i, 1, one).start()
        copy_in(piece(num, 1), i, 2, two).start()
        copy_in(piece(num, 1), i, 3, one).start()
        copy_in(piece(num, 0), i, 3, two).start()
        for e in range(4, half):
            copy_in(chunk(num), i, 4 + e, row_peer(e)).start()
        copy_in(chunk(num), i, 5, partner).start()
        pool(num)

    @pl.loop(0, C - 1)
    def _(i):
        base = others(i) * R
        arrived(i, 1, cut)
        copy_in(piece(base + one, 0), i, 4, two).start()
        arrived(i, 2, cut)
        copy_in(piece(base + two, 1), i, 4, one).start()

    @pl.loop(0, C - 1)
    def _(i):
        base = others(i) * R
        arrived(i, 3, rows)
        copy_in(chunk(base + one), i, 6, partner).start()
        copy_in(chunk(base + two), i, 6, partner).start()
        pool(base + one)
        pool(base + two)

    for d in range(1, C):
        copy_piece((c, part(r)), 0, (r, ctx_peer(d))).start()

    @pl.loop(0, C - 1)
    def _(i):
        base = others(i) * R
        arrived(i, 5, rows)
        process([base + r, base + partner, base + one, base + two])

    @pl.loop(0, C - 1)
    def _(i):
        num = others(i) * R + three
        arrived(i, 4, rows)
        copy_in(chunk(num), i, 7, partner).start()
        for e in range(4, half):
            far = others(i) * R + row_peer(e)
            arrived(i, 4 + e, rows)
            copy_in(chunk(far), i, half + e, partner).start()
            pool(far)
        pool(num)
        pool(others(i) * R + partner)

    pieces_arrived(0, C - 1)
    for e in range(1, half):
        copy_piece((slice(None), part(r)), 1, (row_peer(e), c)).start()
    copy_piece((slice(None), part(r)), 2, (partner, c)).start()

    @pl.loop(0, C - 1)
    def _(i):
        base = others(i) * R
        arrived(i, 6, 2 * rows)
        pool(base + other_row(1))
        pool(base + other_row(2))
        process([base + three, base + other_row(1), base + other_row(2)])

    @pl.loop(0, C - 1)
    def _(i):
        base = others(i) * R
        arrived(i, 7, rows)
        pool(base + other_row(3))
        process([base + other_row(3)])
        for e in range(4, half):
            arrived(i, half + e, rows)
            pool(base + other_row(e))
            process([base + row_peer(e), base + other_row(e)])

    pooled = jnp.concatenate([kpool[i] for i in range(3)], axis=1)
    key_gate = gate(pooled, gk_ref[...])
    logits = fdot(qg, key_gate, ((1,), (1,)))

    maps = jnp.full((PIECE, TB), NEG, jnp.float32)
    for h in range(H):
        pk = peak[h]
        top = jnp.max(pk, axis=0, keepdims=True)
        total = jnp.sum(bsum[h] * jnp.exp(pk - top), axis=0, keepdims=True)
        chance = (pk - (top + jnp.log(total))).T
        for j in range(nb):
            best = jnp.max(chance[j * BLK:(j + 1) * BLK], axis=0, keepdims=True)
            maps = jnp.where(row16 == h * nb + j, best, maps)
    allowed = maps > 0.01 * NEG
    block_map = jnp.where(allowed, jnp.exp(maps), 0.0)
    live = row16 < used
    gate_exp = jnp.where(allowed, jnp.exp(logits), 0.0)
    gate_sum = jnp.where(live, jnp.sum(gate_exp, axis=1, keepdims=True), 1.0)
    map_sum = jnp.where(live, jnp.sum(block_map, axis=1, keepdims=True), 1.0)
    diff = gate_exp / gate_sum - block_map / map_sum
    for h in range(H):
        for j in range(nb):
            diff_own[h:h + 1, j * TB:(j + 1) * TB] = diff[h * nb + j:h * nb + j + 1, :]

    def send(d, e):
        to_row, to_ctx = r + e, c + d
        to_row = jnp.where(to_row >= R, to_row - R, to_row)
        to_ctx = jnp.where(to_ctx >= C, to_ctx - C, to_ctx)
        return pltpu.make_async_remote_copy(
            src_ref=diff_own, dst_ref=diff_all.at[c * R + r],
            send_sem=ds1.at[0], recv_sem=dctx.at[0],
            device_id=(to_row, to_ctx), device_id_type=MESH,
        )

    for e in range(R - 1, -1, -1):
        for d in range(C - 1, -1, -1):
            if d or e:
                send(d, e).start()
    diff_all[c * R + r] = diff_own[...]
    for h in range(H):
        for j in range(nb):
            bm_ref[h, j:j + 1, :] = block_map[h * nb + j:h * nb + j + 1, :]

    pieces_arrived(1, (half - 1) * C)
    for e in range(1, half):
        copy_piece((slice(None), part(row_peer(e))), 2, (partner, c)).start()
    pieces_arrived(2, half * C)

    def gathered(j):
        return jnp.concatenate(
            [pieces[i, pl.ds(j, R, stride=PIECE), :] for i in range(C)], axis=0
        )

    for h in range(H):
        qp = jnp.concatenate([gathered(h * nb + j) for j in range(nb)], axis=0)
        qp_ref[h] = qp
        qg_ref[h] = gate(qp, gq_ref[h])

    for j in range(nb):
        both_ref[j * TB:(j + 1) * TB] = key_gate
    pooled_ref[...] = pooled
    rest = diff_all.at[pl.ds(0, n - 1)]
    pltpu.make_async_copy(rest, rest, dctx.at[0]).wait()
    diff_ref[...] = diff_all[...]
    pltpu.make_async_copy(rest, rest, ds1.at[0]).wait()
    sent = kbuf.at[pl.ds(0, (C - 1) * shard)]
    pltpu.make_async_copy(sent, sent, keysent.at[0]).wait()
    pieces_arrived(3, n - 1)


def finish(map_ref, qp_ref, qg_ref, both_ref, pooled_ref, diff_ref, bm_ref, dq_ref, dk_ref):
    H, nb, TB = map_ref.shape
    bm_ref[...] = map_ref[...]
    both = both_ref[...]
    wide_lane = lax.broadcasted_iota(jnp.int32, (1, nb * TB), 1)
    key_back = jnp.zeros(both.shape, jnp.float32)
    for h in range(H):
        mixed = diff_ref[:, h, :]
        diff = jnp.concatenate(
            [jnp.where(wide_lane // TB == j, mixed, 0.0) for j in range(nb)], axis=0
        )
        back = fdot(diff, both, ((1,), (0,)))
        dq_ref[h] = fdot(qp_ref[h], back, ((0,), (0,)))
        key_back = key_back + fdot(diff, qg_ref[h], ((0,), (0,)))
    folded = key_back[:TB]
    for j in range(1, nb):
        folded = folded + key_back[j * TB:(j + 1) * TB]
    dk_ref[...] = fdot(pooled_ref[...], folded, ((0,), (0,)))


def shards(R, C, queries, keys, doc_ids, gate_query, gate_key):
    H, rows, D = queries.shape
    n = R * C
    nb = rows // BLK
    TB = doc_ids.shape[0]
    half = R // 2
    vm = pl.BlockSpec(memory_space=pltpu.VMEM)
    hbm = pl.BlockSpec(memory_space=pltpu.HBM)
    dma = pltpu.SemaphoreType.DMA
    given = [
        pltpu.with_memory_space_constraint(x, pltpu.HBM)
        for x in (queries, keys, doc_ids, gate_query, gate_key)
    ]
    parts = pl.pallas_call(
        functools.partial(kernel, R, C),
        out_shape=(
            jax.ShapeDtypeStruct((H, nb, TB), jnp.float32),
            jax.ShapeDtypeStruct((H, nb * n, D), jnp.float32),
            jax.ShapeDtypeStruct((H, nb * n, D), jnp.float32),
            jax.ShapeDtypeStruct((nb * TB, D), jnp.float32),
            jax.ShapeDtypeStruct((TB, 3 * D), jnp.float32),
            jax.ShapeDtypeStruct((n, H, nb * TB), jnp.float32),
        ),
        in_specs=[hbm] * 5,
        out_specs=(vm,) * 6,
        scratch_shapes=[
            pltpu.VMEM(queries.shape, queries.dtype),
            pltpu.VMEM(gate_query.shape, gate_query.dtype),
            pltpu.VMEM(gate_key.shape, gate_key.dtype),
            pltpu.SMEM(doc_ids.shape, doc_ids.dtype),
            pltpu.VMEM((C * keys.shape[0], D), jnp.bfloat16),
            pltpu.VMEM((D, H * rows), jnp.bfloat16),
            pltpu.VMEM((H, TB, rows), jnp.float32),
            pltpu.VMEM((H, TB, rows), jnp.float32),
            pltpu.VMEM((3, TB, D), jnp.float32),
            pltpu.VMEM((C, R * PIECE, D), jnp.float32),
            pltpu.VMEM((H, nb * TB), jnp.float32),
            pltpu.VMEM((n, H, nb * TB), jnp.float32),
            dma((5,)), dma((1,)), dma((C - 1, 2 * half)), dma((4,)), dma((1,)), dma((1,)),
        ],
        compiler_params=pltpu.CompilerParams(
            collective_id=0, has_side_effects=True, vmem_limit_bytes=VMEM_LIMIT
        ),
    )(*given)
    return pl.pallas_call(
        finish,
        out_shape=(
            jax.ShapeDtypeStruct((H, nb, TB), jnp.float32),
            jax.ShapeDtypeStruct(gate_query.shape, jnp.float32),
            jax.ShapeDtypeStruct(gate_key.shape, jnp.float32),
        ),
        in_specs=[vm] * 6,
        out_specs=(vm,) * 3,
        compiler_params=pltpu.CompilerParams(vmem_limit_bytes=VMEM_LIMIT),
    )(*parts)


def solution(mesh):
    R, C = mesh.shape["row"], mesh.shape["ctx"]
    in_specs = (P(None, ("row", "ctx"), None), P("ctx", None), P(), P(), P())
    out_specs = (P(None, ("row", "ctx"), None), P(), P())
    return jax.shard_map(
        functools.partial(shards, R, C), mesh=mesh, in_specs=in_specs, out_specs=out_specs,
        check_vma=False,
    )
```

```python
import functools
import math

import jax
import jax.numpy as jnp
from jax import lax
from jax.experimental import pallas as pl
from jax.experimental.pallas import tpu as pltpu
from jax.sharding import PartitionSpec as P

BLK = 64
NEG = -1e30
PIECE = 16
GROUP = 4
MOST = (3, 4)
MESH = pl.DeviceIdType.MESH
VMEM_LIMIT = 32 * 1024 * 1024
HI = lax.Precision.HIGHEST


def fdot(a, b, dims):
    return lax.dot_general(a, b, (dims, ((), ())), precision=HI, preferred_element_type=jnp.float32)


def gate(a, w):
    m = a.shape[0]
    hi = a.astype(jnp.bfloat16)
    rest = a - hi.astype(jnp.float32)
    mid = rest.astype(jnp.bfloat16)
    low = (rest - mid.astype(jnp.float32)).astype(jnp.bfloat16)
    p = jnp.dot(
        jnp.concatenate([hi, mid, low], axis=0), w, preferred_element_type=jnp.float32
    )
    return p[:m] + (p[m:2 * m] + p[2 * m:])


def kernel(
    R, C, q_hbm, k_hbm, doc_hbm, gq_hbm, gk_hbm,
    bm_ref, qp_ref, qg_ref, both_ref, pooled_ref, diff_ref,
    q_ref, gq_ref, gk_ref, doc_ref, kbuf, q_t, peak, bsum, kpool, pieces, diff_own, diff_all,
    local, keysent, rsem, psem, ds1, dctx,
):
    H, rows, D = q_ref.shape
    shard = R * rows
    nb = rows // BLK
    n = R * C
    TB = n * nb
    most = TB * MOST[0] // MOST[1]
    r = lax.axis_index("row")
    c = lax.axis_index("ctx")
    me = r * C + c
    half = R // 2
    scale = 1.0 / math.sqrt(D)
    used = H * nb
    cut = rows // 2

    def ctx_peer(d):
        return lax.rem(c + d, C)

    def flip(rr, e):
        bit = 2
        while e:
            if e % 2:
                rr = rr + bit - 2 * bit * lax.rem(rr // bit, 2)
            e, bit = e // 2, bit * 2
        return rr

    def row_peer(e):
        return flip(r, e)

    partner = r + 1 - 2 * lax.rem(r, 2)

    def other_row(e):
        return flip(partner, e)

    def others(i):
        return jnp.where(i >= c, i + 1, i)

    def far_first(i):
        down = C - 1 - i
        return jnp.where(2 * c < C, jnp.where(down <= c, down - 1, down), others(i))

    barrier = pltpu.get_barrier_semaphore()
    for d in range(1, C):
        pl.semaphore_signal(barrier, inc=1, device_id=(r, ctx_peer(d)), device_id_type=MESH)
    for e in range(1, half):
        pl.semaphore_signal(barrier, inc=1, device_id=(row_peer(e), c), device_id_type=MESH)
    pl.semaphore_signal(barrier, inc=1, device_id=(partner, c), device_id_type=MESH)

    def chunk(num):
        return pl.ds(pl.multiple_of(num * rows, rows), rows)

    def piece(num, x):
        return pl.ds(pl.multiple_of(num * rows + x * cut, cut), cut)

    def part(rr):
        return pl.ds(pl.multiple_of(rr * PIECE, PIECE), used)

    loads = [
        pltpu.make_async_copy(q_hbm, q_ref, local.at[0]),
        pltpu.make_async_copy(
            k_hbm, kbuf.at[pl.ds(pl.multiple_of(c * shard, shard), shard)], local.at[1]
        ),
        pltpu.make_async_copy(doc_hbm, doc_ref, local.at[2]),
        pltpu.make_async_copy(gq_hbm, gq_ref, local.at[3]),
        pltpu.make_async_copy(gk_hbm, gk_ref, local.at[4]),
    ]
    for load in loads:
        load.start()
    pl.semaphore_wait(barrier, C - 1 + half)

    def place(at, cc):
        return jnp.where(at < cc, at, at - 1)

    def copy_ctx(cc):
        return pltpu.make_async_remote_copy(
            src_ref=k_hbm.at[pl.ds(pl.multiple_of(r * rows, rows), rows)],
            dst_ref=kbuf.at[chunk(c * R + r)],
            send_sem=keysent.at[0], recv_sem=rsem.at[place(c, cc), 0],
            device_id=(r, cc), device_id_type=MESH,
        )

    def copy_in(at, p, kind, to):
        return pltpu.make_async_remote_copy(
            src_ref=kbuf.at[at], dst_ref=kbuf.at[at],
            send_sem=keysent.at[0], recv_sem=rsem.at[p, kind],
            device_id=(to, c), device_id_type=MESH,
        )

    def arrived(p, kind, size):
        at = kbuf.at[pl.ds(0, size)]
        pltpu.make_async_copy(at, at, rsem.at[p, kind]).wait()

    def copy_piece(at, kind, device):
        return pltpu.make_async_remote_copy(
            src_ref=pieces.at[at], dst_ref=pieces.at[at],
            send_sem=psem.at[3], recv_sem=psem.at[kind],
            device_id=device, device_id_type=MESH,
        )

    def pieces_arrived(kind, count):
        at = kbuf.at[pl.ds(0, 2 * used * count)]
        pltpu.make_async_copy(at, at, psem.at[kind]).wait()

    @pl.loop(0, C - 1)
    def _(i):
        copy_ctx(far_first(i)).start()

    peak[...] = jnp.full_like(peak, NEG)
    bsum[...] = jnp.zeros_like(bsum)
    loads[0].wait()
    for h in range(H):
        qf = q_ref[h].astype(jnp.float32)
        q_t[:, h * rows:(h + 1) * rows] = qf.T.astype(jnp.bfloat16)
        for j in range(nb):
            pieces[c, pl.ds(r * PIECE + h * nb + j, 1), :] = jnp.mean(
                qf[j * BLK:(j + 1) * BLK], axis=0, keepdims=True
            )

    loads[2].wait()
    a0 = me * nb
    lane = lax.broadcasted_iota(jnp.int32, (1, 2 * rows), 1)
    qdoc = jnp.zeros((1, 2 * rows), jnp.int32)
    for j in range(nb):
        qdoc = jnp.where(lax.rem(lane, rows) // BLK == j, doc_ref[a0 + j], qdoc)

    def score(nums, masked):
        keys = jnp.concatenate([kbuf[chunk(num), :] for num in nums], axis=0)
        for h in range(0, H, 2):
            width = min(2, H - h) * rows
            cols = slice(h * rows, h * rows + width)
            s = jnp.dot(keys, q_t[:, cols], preferred_element_type=jnp.float32)
            if masked:
                ki = lax.broadcasted_iota(jnp.int32, s.shape, 0)
                qi = lax.rem(lax.broadcasted_iota(jnp.int32, s.shape, 1), rows)
                s = jnp.where(ki - qi <= (me - nums[0]) * rows, s, NEG)
            for m, num in enumerate(nums):
                for j in range(nb):
                    b = num * nb + j
                    at = (m * nb + j) * BLK
                    t = s[at:at + BLK]
                    top = jnp.max(t, axis=0, keepdims=True)
                    total = jnp.sum(
                        jnp.exp2((t - top) * (scale * math.log2(math.e))), axis=0, keepdims=True
                    )
                    top = jnp.where(qdoc[:, :width] == doc_ref[b], top * scale, NEG)
                    for k in range(width // rows):
                        peak[h + k, pl.ds(b, 1), :] = top[:, k * rows:(k + 1) * rows]
                        bsum[h + k, pl.ds(b, 1), :] = total[:, k * rows:(k + 1) * rows]

    def pool(num):
        wide = kbuf[chunk(num), :].astype(jnp.float32)
        for j in range(nb):
            t = wide[j * BLK:(j + 1) * BLK]
            for i, how in enumerate((jnp.max, jnp.min, jnp.mean)):
                kpool[i, pl.ds(num * nb + j, 1), :] = how(t, axis=0, keepdims=True)

    def near(num):
        return (num + 1) * nb - 1 + most > a0

    def process(nums):
        whole = (nums[0] < me) & near(nums[0])
        for num in nums[1:]:
            whole = whole & (num < me) & near(num)

        @pl.when(whole)
        def _():
            for i in range(0, len(nums), 2):
                score(nums[i:i + 2], False)

        @pl.when(jnp.logical_not(whole))
        def _():
            for num in nums:
                @pl.when((num <= me) & near(num))
                def _():
                    score([num], True)

    loads[1].wait()

    @pl.loop(0, half)
    def _(g):
        pool(c * R + 2 * g)
        pool(c * R + 2 * g + 1)
        process([c * R + 2 * g, c * R + 2 * g + 1])

    loads[3].wait()
    loads[4].wait()
    row16 = lax.broadcasted_iota(jnp.int32, (PIECE, 1), 0)
    own = jnp.where(row16 < used, pieces[c, pl.ds(pl.multiple_of(r * PIECE, PIECE), PIECE), :], 0.0)
    qg = jnp.zeros((PIECE, D), jnp.float32)
    for h in range(H):
        qg = jnp.where(row16 // nb == h, gate(own, gq_ref[h]), qg)

    one, two, three = (row_peer(e) for e in (1, 2, 3))

    @pl.loop(0, C - 1)
    def _(i):
        num = others(i) * R + r
        arrived(i, 0, rows)
        copy_in(piece(num, 0), i, 1, one).start()
        copy_in(piece(num, 1), i, 2, two).start()
        copy_in(chunk(num), i, 5, partner).start()

    @pl.loop(0, C - 1)
    def _(i):
        num = others(i) * R + r
        copy_in(piece(num, 1), i, 3, one).start()
        copy_in(piece(num, 0), i, 3, two).start()
        for e in range(4, half):
            copy_in(chunk(num), i, 4 + e, row_peer(e)).start()
        pool(num)

    @pl.loop(0, C - 1)
    def _(i):
        base = others(i) * R
        arrived(i, 1, cut)
        copy_in(piece(base + one, 0), i, 4, two).start()
        arrived(i, 2, cut)
        copy_in(piece(base + two, 1), i, 4, one).start()

    @pl.loop(0, C - 1)
    def _(i):
        base = others(i) * R
        arrived(i, 3, rows)
        copy_in(chunk(base + one), i, 6, partner).start()
        copy_in(chunk(base + two), i, 6, partner).start()
        pool(base + one)
        pool(base + two)

    for d in range(1, C):
        copy_piece((c, part(r)), 0, (r, ctx_peer(d))).start()

    @pl.loop(0, C - 1)
    def _(i):
        base = others(i) * R
        arrived(i, 5, rows)
        process([base + r, base + partner, base + one, base + two])

    @pl.loop(0, C - 1)
    def _(i):
        num = others(i) * R + three
        arrived(i, 4, rows)
        copy_in(chunk(num), i, 7, partner).start()
        for e in range(4, half):
            far = others(i) * R + row_peer(e)
            arrived(i, 4 + e, rows)
            copy_in(chunk(far), i, half + e, partner).start()
            pool(far)
        pool(num)
        pool(others(i) * R + partner)

    pieces_arrived(0, C - 1)
    for e in range(1, half):
        copy_piece((slice(None), part(r)), 1, (row_peer(e), c)).start()
    copy_piece((slice(None), part(r)), 2, (partner, c)).start()

    @pl.loop(0, C - 1)
    def _(i):
        base = others(i) * R
        arrived(i, 6, 2 * rows)
        pool(base + other_row(1))
        pool(base + other_row(2))
        process([base + three, base + other_row(1), base + other_row(2)])

    @pl.loop(0, C - 1)
    def _(i):
        base = others(i) * R
        arrived(i, 7, rows)
        pool(base + other_row(3))
        process([base + other_row(3)])
        for e in range(4, half):
            arrived(i, half + e, rows)
            pool(base + other_row(e))
            process([base + row_peer(e), base + other_row(e)])

    pooled = jnp.concatenate([kpool[i] for i in range(3)], axis=1)
    key_gate = gate(pooled, gk_ref[...])
    logits = fdot(qg, key_gate, ((1,), (1,)))

    maps = jnp.full((PIECE, TB), NEG, jnp.float32)
    for h in range(H):
        pk = peak[h]
        top = jnp.max(pk, axis=0, keepdims=True)
        total = jnp.sum(bsum[h] * jnp.exp(pk - top), axis=0, keepdims=True)
        chance = (pk - (top + jnp.log(total))).T
        for j in range(nb):
            best = jnp.max(chance[j * BLK:(j + 1) * BLK], axis=0, keepdims=True)
            maps = jnp.where(row16 == h * nb + j, best, maps)
    allowed = maps > 0.01 * NEG
    block_map = jnp.where(allowed, jnp.exp(maps), 0.0)
    live = row16 < used
    gate_exp = jnp.where(allowed, jnp.exp(logits), 0.0)
    gate_sum = jnp.where(live, jnp.sum(gate_exp, axis=1, keepdims=True), 1.0)
    map_sum = jnp.where(live, jnp.sum(block_map, axis=1, keepdims=True), 1.0)
    diff = gate_exp / gate_sum - block_map / map_sum
    for h in range(H):
        for j in range(nb):
            diff_own[h:h + 1, j * TB:(j + 1) * TB] = diff[h * nb + j:h * nb + j + 1, :]

    def send(d, e):
        to_row, to_ctx = r + e, c + d
        to_row = jnp.where(to_row >= R, to_row - R, to_row)
        to_ctx = jnp.where(to_ctx >= C, to_ctx - C, to_ctx)
        return pltpu.make_async_remote_copy(
            src_ref=diff_own, dst_ref=diff_all.at[c * R + r],
            send_sem=ds1.at[0], recv_sem=dctx.at[0],
            device_id=(to_row, to_ctx), device_id_type=MESH,
        )

    for e in range(R - 1, -1, -1):
        for d in range(C - 1, -1, -1):
            if d or e:
                send(d, e).start()
    diff_all[c * R + r] = diff_own[...]
    for h in range(H):
        for j in range(nb):
            bm_ref[h, j:j + 1, :] = block_map[h * nb + j:h * nb + j + 1, :]

    pieces_arrived(1, (half - 1) * C)
    for e in range(1, half):
        copy_piece((slice(None), part(row_peer(e))), 2, (partner, c)).start()
    pieces_arrived(2, half * C)

    def gathered(j):
        return jnp.concatenate(
            [pieces[i, pl.ds(j, R, stride=PIECE), :] for i in range(C)], axis=0
        )

    for h in range(H):
        qp = jnp.concatenate([gathered(h * nb + j) for j in range(nb)], axis=0)
        qp_ref[h] = qp.T
        qg = gate(qp, gq_ref[h])
        for j in range(nb):
            qg_ref[h * n:(h + 1) * n, j * D:(j + 1) * D] = qg[j * n:(j + 1) * n]

    both_ref[...] = jnp.zeros_like(both_ref)
    for j in range(nb):
        both_ref[j * TB:(j + 1) * TB, j * D:(j + 1) * D] = key_gate
    for i in range(3):
        pooled_ref[i * D:(i + 1) * D] = kpool[i].T
    rest = diff_all.at[pl.ds(0, n - 1)]
    pltpu.make_async_copy(rest, rest, dctx.at[0]).wait()
    for h in range(H):
        diff_ref[h * n:(h + 1) * n] = diff_all[:, h, :]
    pltpu.make_async_copy(rest, rest, ds1.at[0]).wait()
    sent = kbuf.at[pl.ds(0, (C - 1) * shard)]
    pltpu.make_async_copy(sent, sent, keysent.at[0]).wait()
    pieces_arrived(3, n - 1)


def finish(
    map_ref, qp_ref, qg_ref, both_ref, pooled_ref, diff_ref, bm_hbm, dq_hbm, dk_hbm,
    dq_ref, dk_ref, sem,
):
    H, nb, TB = map_ref.shape
    D = dq_ref.shape[-1]
    n = diff_ref.shape[0] // H
    out = pltpu.make_async_copy(map_ref, bm_hbm, sem.at[0])
    out.start()
    mixed = diff_ref[...]
    spread = fdot(mixed, qg_ref[...], ((0,), (0,)))
    folded = spread[:TB, :D]
    for j in range(1, nb):
        folded = folded + spread[j * TB:(j + 1) * TB, j * D:(j + 1) * D]
    back = fdot(mixed, both_ref[...], ((1,), (0,)))
    dk_ref[...] = fdot(pooled_ref[...], folded, ((1,), (0,)))
    keys_out = pltpu.make_async_copy(dk_ref, dk_hbm, sem.at[1])
    keys_out.start()
    for h in range(H):
        rows = slice(h * n, (h + 1) * n)
        own = jnp.concatenate([back[rows, j * D:(j + 1) * D] for j in range(nb)], axis=0)
        dq_ref[h] = fdot(qp_ref[h], own, ((1,), (0,)))
        pltpu.make_async_copy(dq_ref.at[h], dq_hbm.at[h], sem.at[2]).start()
    out.wait()
    keys_out.wait()
    pltpu.make_async_copy(dq_ref, dq_hbm, sem.at[2]).wait()


def shards(R, C, queries, keys, doc_ids, gate_query, gate_key):
    H, rows, D = queries.shape
    n = R * C
    nb = rows // BLK
    TB = doc_ids.shape[0]
    half = R // 2
    vm = pl.BlockSpec(memory_space=pltpu.VMEM)
    hbm = pl.BlockSpec(memory_space=pltpu.HBM)
    dma = pltpu.SemaphoreType.DMA
    given = [
        pltpu.with_memory_space_constraint(x, pltpu.HBM)
        for x in (queries, keys, doc_ids, gate_query, gate_key)
    ]
    parts = pl.pallas_call(
        functools.partial(kernel, R, C),
        out_shape=(
            jax.ShapeDtypeStruct((H, nb, TB), jnp.float32),
            jax.ShapeDtypeStruct((H, D, nb * n), jnp.float32),
            jax.ShapeDtypeStruct((H * n, nb * D), jnp.float32),
            jax.ShapeDtypeStruct((nb * TB, nb * D), jnp.float32),
            jax.ShapeDtypeStruct((3 * D, TB), jnp.float32),
            jax.ShapeDtypeStruct((H * n, nb * TB), jnp.float32),
        ),
        in_specs=[hbm] * 5,
        out_specs=(vm,) * 6,
        scratch_shapes=[
            pltpu.VMEM(queries.shape, queries.dtype),
            pltpu.VMEM(gate_query.shape, gate_query.dtype),
            pltpu.VMEM(gate_key.shape, gate_key.dtype),
            pltpu.SMEM(doc_ids.shape, doc_ids.dtype),
            pltpu.VMEM((C * keys.shape[0], D), jnp.bfloat16),
            pltpu.VMEM((D, H * rows), jnp.bfloat16),
            pltpu.VMEM((H, TB, rows), jnp.float32),
            pltpu.VMEM((H, TB, rows), jnp.float32),
            pltpu.VMEM((3, TB, D), jnp.float32),
            pltpu.VMEM((C, R * PIECE, D), jnp.float32),
            pltpu.VMEM((H, nb * TB), jnp.float32),
            pltpu.VMEM((n, H, nb * TB), jnp.float32),
            dma((5,)), dma((1,)), dma((C - 1, 2 * half)), dma((4,)), dma((1,)), dma((1,)),
        ],
        compiler_params=pltpu.CompilerParams(
            collective_id=0, has_side_effects=True, vmem_limit_bytes=VMEM_LIMIT
        ),
    )(*given)
    return pl.pallas_call(
        finish,
        out_shape=(
            jax.ShapeDtypeStruct((H, nb, TB), jnp.float32),
            jax.ShapeDtypeStruct(gate_query.shape, jnp.float32),
            jax.ShapeDtypeStruct(gate_key.shape, jnp.float32),
        ),
        in_specs=[vm] * 6,
        out_specs=(hbm,) * 3,
        scratch_shapes=[
            pltpu.VMEM(gate_query.shape, jnp.float32),
            pltpu.VMEM(gate_key.shape, jnp.float32),
            dma((3,)),
        ],
        compiler_params=pltpu.CompilerParams(vmem_limit_bytes=VMEM_LIMIT),
    )(*parts)


def solution(mesh):
    R, C = mesh.shape["row"], mesh.shape["ctx"]
    in_specs = (P(None, ("row", "ctx"), None), P("ctx", None), P(), P(), P())
    out_specs = (P(None, ("row", "ctx"), None), P(), P())
    return jax.shard_map(
        functools.partial(shards, R, C), mesh=mesh, in_specs=in_specs, out_specs=out_specs,
        check_vma=False,
    )
```

```python
import functools
import math

import jax
import jax.numpy as jnp
from jax import lax
from jax.experimental import pallas as pl
from jax.experimental.pallas import tpu as pltpu
from jax.sharding import PartitionSpec as P

BLK = 64
NEG = -1e30
PIECE = 16
GROUP = 4
MOST = (3, 4)
MESH = pl.DeviceIdType.MESH
VMEM_LIMIT = 32 * 1024 * 1024
HI = lax.Precision.HIGHEST


def fdot(a, b, dims):
    return lax.dot_general(a, b, (dims, ((), ())), precision=HI, preferred_element_type=jnp.float32)


def gate(a, w):
    m = a.shape[0]
    hi = a.astype(jnp.bfloat16)
    rest = a - hi.astype(jnp.float32)
    mid = rest.astype(jnp.bfloat16)
    low = (rest - mid.astype(jnp.float32)).astype(jnp.bfloat16)
    p = jnp.dot(
        jnp.concatenate([hi, mid, low], axis=0), w, preferred_element_type=jnp.float32
    )
    return p[:m] + (p[m:2 * m] + p[2 * m:])


def kernel(
    R, C, q_hbm, k_hbm, doc_hbm, gq_hbm, gk_hbm,
    bm_ref, qp_ref, qg_ref, both_ref, pooled_ref, diff_ref,
    q_ref, gq_ref, gk_ref, doc_ref, kbuf, q_t, peak, bsum, kpool, pieces, diff_own, diff_all,
    local, keysent, rsem, psem, ds1, dctx,
):
    H, rows, D = q_ref.shape
    shard = R * rows
    nb = rows // BLK
    n = R * C
    TB = n * nb
    most = TB * MOST[0] // MOST[1]
    r = lax.axis_index("row")
    c = lax.axis_index("ctx")
    me = r * C + c
    half = R // 2
    scale = 1.0 / math.sqrt(D)
    used = H * nb
    cut = rows // 2

    def ctx_peer(d):
        return lax.rem(c + d, C)

    def flip(rr, e):
        bit = 2
        while e:
            if e % 2:
                rr = rr + bit - 2 * bit * lax.rem(rr // bit, 2)
            e, bit = e // 2, bit * 2
        return rr

    def row_peer(e):
        return flip(r, e)

    partner = r + 1 - 2 * lax.rem(r, 2)

    def other_row(e):
        return flip(partner, e)

    def others(i):
        return jnp.where(i >= c, i + 1, i)

    def far_first(i):
        down = C - 1 - i
        return jnp.where(2 * c < C, jnp.where(down <= c, down - 1, down), others(i))

    barrier = pltpu.get_barrier_semaphore()
    for d in range(1, C):
        pl.semaphore_signal(barrier, inc=1, device_id=(r, ctx_peer(d)), device_id_type=MESH)
    for e in range(1, half):
        pl.semaphore_signal(barrier, inc=1, device_id=(row_peer(e), c), device_id_type=MESH)
    pl.semaphore_signal(barrier, inc=1, device_id=(partner, c), device_id_type=MESH)

    def chunk(num):
        return pl.ds(pl.multiple_of(num * rows, rows), rows)

    def piece(num, x):
        return pl.ds(pl.multiple_of(num * rows + x * cut, cut), cut)

    def part(rr):
        return pl.ds(pl.multiple_of(rr * PIECE, PIECE), used)

    loads = [
        pltpu.make_async_copy(q_hbm, q_ref, local.at[0]),
        pltpu.make_async_copy(
            k_hbm, kbuf.at[pl.ds(pl.multiple_of(c * shard, shard), shard)], local.at[1]
        ),
        pltpu.make_async_copy(doc_hbm, doc_ref, local.at[2]),
        pltpu.make_async_copy(gq_hbm, gq_ref, local.at[3]),
        pltpu.make_async_copy(gk_hbm, gk_ref, local.at[4]),
    ]
    for load in loads:
        load.start()
    pl.semaphore_wait(barrier, C - 1 + half)

    def place(at, cc):
        return jnp.where(at < cc, at, at - 1)

    def copy_ctx(cc):
        return pltpu.make_async_remote_copy(
            src_ref=k_hbm.at[pl.ds(pl.multiple_of(r * rows, rows), rows)],
            dst_ref=kbuf.at[chunk(c * R + r)],
            send_sem=keysent.at[0], recv_sem=rsem.at[place(c, cc), 0],
            device_id=(r, cc), device_id_type=MESH,
        )

    def copy_in(at, p, kind, to):
        return pltpu.make_async_remote_copy(
            src_ref=kbuf.at[at], dst_ref=kbuf.at[at],
            send_sem=keysent.at[0], recv_sem=rsem.at[p, kind],
            device_id=(to, c), device_id_type=MESH,
        )

    def arrived(p, kind, size):
        at = kbuf.at[pl.ds(0, size)]
        pltpu.make_async_copy(at, at, rsem.at[p, kind]).wait()

    def copy_piece(at, kind, device):
        return pltpu.make_async_remote_copy(
            src_ref=pieces.at[at], dst_ref=pieces.at[at],
            send_sem=psem.at[3], recv_sem=psem.at[kind],
            device_id=device, device_id_type=MESH,
        )

    def pieces_arrived(kind, count):
        at = kbuf.at[pl.ds(0, 2 * used * count)]
        pltpu.make_async_copy(at, at, psem.at[kind]).wait()

    @pl.loop(0, C - 1)
    def _(i):
        copy_ctx(far_first(i)).start()

    peak[...] = jnp.full_like(peak, NEG)
    bsum[...] = jnp.zeros_like(bsum)
    loads[0].wait()
    for h in range(H):
        qf = q_ref[h].astype(jnp.float32)
        q_t[:, h * rows:(h + 1) * rows] = qf.T.astype(jnp.bfloat16)
        for j in range(nb):
            pieces[c, pl.ds(r * PIECE + h * nb + j, 1), :] = jnp.mean(
                qf[j * BLK:(j + 1) * BLK], axis=0, keepdims=True
            )

    loads[2].wait()
    a0 = me * nb
    lane = lax.broadcasted_iota(jnp.int32, (1, 2 * rows), 1)
    qdoc = jnp.zeros((1, 2 * rows), jnp.int32)
    for j in range(nb):
        qdoc = jnp.where(lax.rem(lane, rows) // BLK == j, doc_ref[a0 + j], qdoc)

    def score(nums, masked):
        keys = jnp.concatenate([kbuf[chunk(num), :] for num in nums], axis=0)
        for h in range(0, H, 2):
            width = min(2, H - h) * rows
            cols = slice(h * rows, h * rows + width)
            s = jnp.dot(keys, q_t[:, cols], preferred_element_type=jnp.float32)
            if masked:
                ki = lax.broadcasted_iota(jnp.int32, s.shape, 0)
                qi = lax.rem(lax.broadcasted_iota(jnp.int32, s.shape, 1), rows)
                s = jnp.where(ki - qi <= (me - nums[0]) * rows, s, NEG)
            for m, num in enumerate(nums):
                for j in range(nb):
                    b = num * nb + j
                    at = (m * nb + j) * BLK
                    t = s[at:at + BLK]
                    top = jnp.max(t, axis=0, keepdims=True)
                    total = jnp.sum(
                        jnp.exp2((t - top) * (scale * math.log2(math.e))), axis=0, keepdims=True
                    )
                    top = jnp.where(qdoc[:, :width] == doc_ref[b], top * scale, NEG)
                    for k in range(width // rows):
                        peak[h + k, pl.ds(b, 1), :] = top[:, k * rows:(k + 1) * rows]
                        bsum[h + k, pl.ds(b, 1), :] = total[:, k * rows:(k + 1) * rows]

    def pool(num):
        wide = kbuf[chunk(num), :].astype(jnp.float32)
        for j in range(nb):
            t = wide[j * BLK:(j + 1) * BLK]
            for i, how in enumerate((jnp.max, jnp.min, jnp.mean)):
                kpool[i, pl.ds(num * nb + j, 1), :] = how(t, axis=0, keepdims=True)

    def near(num):
        return (num + 1) * nb - 1 + most > a0

    def process(nums):
        whole = (nums[0] < me) & near(nums[0])
        for num in nums[1:]:
            whole = whole & (num < me) & near(num)

        @pl.when(whole)
        def _():
            for i in range(0, len(nums), 2):
                score(nums[i:i + 2], False)

        @pl.when(jnp.logical_not(whole))
        def _():
            for num in nums:
                @pl.when((num <= me) & near(num))
                def _():
                    score([num], True)

    loads[1].wait()

    @pl.loop(0, half)
    def _(g):
        pool(c * R + 2 * g)
        pool(c * R + 2 * g + 1)
        process([c * R + 2 * g, c * R + 2 * g + 1])

    loads[3].wait()
    loads[4].wait()
    row16 = lax.broadcasted_iota(jnp.int32, (PIECE, 1), 0)
    own = jnp.where(row16 < used, pieces[c, pl.ds(pl.multiple_of(r * PIECE, PIECE), PIECE), :], 0.0)
    qg = jnp.zeros((PIECE, D), jnp.float32)
    for h in range(H):
        qg = jnp.where(row16 // nb == h, gate(own, gq_ref[h]), qg)

    one, two, three = (row_peer(e) for e in (1, 2, 3))

    @pl.loop(0, C - 1)
    def _(i):
        num = others(i) * R + r
        arrived(i, 0, rows)
        copy_in(piece(num, 0), i, 1, one).start()
        copy_in(piece(num, 1), i, 2, two).start()
        copy_in(chunk(num), i, 5, partner).start()

    @pl.loop(0, C - 1)
    def _(i):
        num = others(i) * R + r
        copy_in(piece(num, 1), i, 3, one).start()
        copy_in(piece(num, 0), i, 3, two).start()
        for e in range(4, half):
            copy_in(chunk(num), i, 4 + e, row_peer(e)).start()
        pool(num)

    @pl.loop(0, C - 1)
    def _(i):
        base = others(i) * R
        arrived(i, 1, cut)
        copy_in(piece(base + one, 0), i, 4, two).start()
        arrived(i, 2, cut)
        copy_in(piece(base + two, 1), i, 4, one).start()

    @pl.loop(0, C - 1)
    def _(i):
        base = others(i) * R
        arrived(i, 3, rows)
        copy_in(chunk(base + one), i, 6, partner).start()
        copy_in(chunk(base + two), i, 6, partner).start()
        pool(base + one)
        pool(base + two)

    for d in range(1, C):
        copy_piece((c, part(r)), 0, (r, ctx_peer(d))).start()

    @pl.loop(0, C - 1)
    def _(i):
        base = others(i) * R
        arrived(i, 5, rows)
        process([base + r, base + partner, base + one, base + two])

    @pl.loop(0, C - 1)
    def _(i):
        base = others(i) * R
        arrived(i, 6, 2 * rows)
        pool(base + other_row(1))
        pool(base + other_row(2))
        process([base + other_row(1), base + other_row(2)])

    @pl.loop(0, C - 1)
    def _(i):
        num = others(i) * R + three
        arrived(i, 4, rows)
        copy_in(chunk(num), i, 7, partner).start()
        for e in range(4, half):
            far = others(i) * R + row_peer(e)
            arrived(i, 4 + e, rows)
            copy_in(chunk(far), i, half + e, partner).start()
            pool(far)
        pool(num)
        pool(others(i) * R + partner)

    pieces_arrived(0, C - 1)
    for e in range(1, half):
        copy_piece((slice(None), part(r)), 1, (row_peer(e), c)).start()
    copy_piece((slice(None), part(r)), 2, (partner, c)).start()

    @pl.loop(0, C - 1)
    def _(i):
        process([others(i) * R + three])

    @pl.loop(0, C - 1)
    def _(i):
        base = others(i) * R
        arrived(i, 7, rows)
        pool(base + other_row(3))
        process([base + other_row(3)])
        for e in range(4, half):
            arrived(i, half + e, rows)
            pool(base + other_row(e))
            process([base + row_peer(e), base + other_row(e)])

    pooled = jnp.concatenate([kpool[i] for i in range(3)], axis=1)
    key_gate = gate(pooled, gk_ref[...])
    logits = fdot(qg, key_gate, ((1,), (1,)))

    maps = jnp.full((PIECE, TB), NEG, jnp.float32)
    for h in range(H):
        pk = peak[h]
        top = jnp.max(pk, axis=0, keepdims=True)
        total = jnp.sum(bsum[h] * jnp.exp(pk - top), axis=0, keepdims=True)
        chance = (pk - (top + jnp.log(total))).T
        for j in range(nb):
            best = jnp.max(chance[j * BLK:(j + 1) * BLK], axis=0, keepdims=True)
            maps = jnp.where(row16 == h * nb + j, best, maps)
    allowed = maps > 0.01 * NEG
    block_map = jnp.where(allowed, jnp.exp(maps), 0.0)
    live = row16 < used
    gate_exp = jnp.where(allowed, jnp.exp(logits), 0.0)
    gate_sum = jnp.where(live, jnp.sum(gate_exp, axis=1, keepdims=True), 1.0)
    map_sum = jnp.where(live, jnp.sum(block_map, axis=1, keepdims=True), 1.0)
    diff = gate_exp / gate_sum - block_map / map_sum
    for h in range(H):
        for j in range(nb):
            diff_own[h:h + 1, j * TB:(j + 1) * TB] = diff[h * nb + j:h * nb + j + 1, :]

    def send(d, e):
        to_row, to_ctx = r + e, c + d
        to_row = jnp.where(to_row >= R, to_row - R, to_row)
        to_ctx = jnp.where(to_ctx >= C, to_ctx - C, to_ctx)
        return pltpu.make_async_remote_copy(
            src_ref=diff_own, dst_ref=diff_all.at[c * R + r],
            send_sem=ds1.at[0], recv_sem=dctx.at[0],
            device_id=(to_row, to_ctx), device_id_type=MESH,
        )

    for e in range(R - 1, -1, -1):
        for d in range(C - 1, -1, -1):
            if d or e:
                send(d, e).start()
    diff_all[c * R + r] = diff_own[...]
    for h in range(H):
        for j in range(nb):
            bm_ref[h, j:j + 1, :] = block_map[h * nb + j:h * nb + j + 1, :]

    pieces_arrived(1, (half - 1) * C)
    for e in range(1, half):
        copy_piece((slice(None), part(row_peer(e))), 2, (partner, c)).start()
    pieces_arrived(2, half * C)

    def gathered(j):
        return jnp.concatenate(
            [pieces[i, pl.ds(j, R, stride=PIECE), :] for i in range(C)], axis=0
        )

    for h in range(H):
        qp = jnp.concatenate([gathered(h * nb + j) for j in range(nb)], axis=0)
        qp_ref[h] = qp.T
        qg = gate(qp, gq_ref[h])
        for j in range(nb):
            qg_ref[h * n:(h + 1) * n, j * D:(j + 1) * D] = qg[j * n:(j + 1) * n]

    both_ref[...] = jnp.zeros_like(both_ref)
    for j in range(nb):
        both_ref[j * TB:(j + 1) * TB, j * D:(j + 1) * D] = key_gate
    for i in range(3):
        pooled_ref[i * D:(i + 1) * D] = kpool[i].T
    rest = diff_all.at[pl.ds(0, n - 1)]
    pltpu.make_async_copy(rest, rest, dctx.at[0]).wait()
    for h in range(H):
        diff_ref[h * n:(h + 1) * n] = diff_all[:, h, :]
    pltpu.make_async_copy(rest, rest, ds1.at[0]).wait()
    sent = kbuf.at[pl.ds(0, (C - 1) * shard)]
    pltpu.make_async_copy(sent, sent, keysent.at[0]).wait()
    pieces_arrived(3, n - 1)


def finish(
    map_ref, qp_ref, qg_ref, both_ref, pooled_ref, diff_ref, bm_hbm, dq_hbm, dk_hbm,
    dq_ref, dk_ref, sem,
):
    H, nb, TB = map_ref.shape
    D = dq_ref.shape[-1]
    n = diff_ref.shape[0] // H
    out = pltpu.make_async_copy(map_ref, bm_hbm, sem.at[0])
    out.start()
    mixed = diff_ref[...]
    spread = fdot(mixed, qg_ref[...], ((0,), (0,)))
    folded = spread[:TB, :D]
    for j in range(1, nb):
        folded = folded + spread[j * TB:(j + 1) * TB, j * D:(j + 1) * D]
    back = fdot(mixed, both_ref[...], ((1,), (0,)))
    dk_ref[...] = fdot(pooled_ref[...], folded, ((1,), (0,)))
    keys_out = pltpu.make_async_copy(dk_ref, dk_hbm, sem.at[1])
    keys_out.start()
    for h in range(H):
        rows = slice(h * n, (h + 1) * n)
        own = jnp.concatenate([back[rows, j * D:(j + 1) * D] for j in range(nb)], axis=0)
        dq_ref[h] = fdot(qp_ref[h], own, ((1,), (0,)))
        pltpu.make_async_copy(dq_ref.at[h], dq_hbm.at[h], sem.at[2]).start()
    out.wait()
    keys_out.wait()
    pltpu.make_async_copy(dq_ref, dq_hbm, sem.at[2]).wait()


def shards(R, C, queries, keys, doc_ids, gate_query, gate_key):
    H, rows, D = queries.shape
    n = R * C
    nb = rows // BLK
    TB = doc_ids.shape[0]
    half = R // 2
    vm = pl.BlockSpec(memory_space=pltpu.VMEM)
    hbm = pl.BlockSpec(memory_space=pltpu.HBM)
    dma = pltpu.SemaphoreType.DMA
    given = [
        pltpu.with_memory_space_constraint(x, pltpu.HBM)
        for x in (queries, keys, doc_ids, gate_query, gate_key)
    ]
    parts = pl.pallas_call(
        functools.partial(kernel, R, C),
        out_shape=(
            jax.ShapeDtypeStruct((H, nb, TB), jnp.float32),
            jax.ShapeDtypeStruct((H, D, nb * n), jnp.float32),
            jax.ShapeDtypeStruct((H * n, nb * D), jnp.float32),
            jax.ShapeDtypeStruct((nb * TB, nb * D), jnp.float32),
            jax.ShapeDtypeStruct((3 * D, TB), jnp.float32),
            jax.ShapeDtypeStruct((H * n, nb * TB), jnp.float32),
        ),
        in_specs=[hbm] * 5,
        out_specs=(vm,) * 6,
        scratch_shapes=[
            pltpu.VMEM(queries.shape, queries.dtype),
            pltpu.VMEM(gate_query.shape, gate_query.dtype),
            pltpu.VMEM(gate_key.shape, gate_key.dtype),
            pltpu.SMEM(doc_ids.shape, doc_ids.dtype),
            pltpu.VMEM((C * keys.shape[0], D), jnp.bfloat16),
            pltpu.VMEM((D, H * rows), jnp.bfloat16),
            pltpu.VMEM((H, TB, rows), jnp.float32),
            pltpu.VMEM((H, TB, rows), jnp.float32),
            pltpu.VMEM((3, TB, D), jnp.float32),
            pltpu.VMEM((C, R * PIECE, D), jnp.float32),
            pltpu.VMEM((H, nb * TB), jnp.float32),
            pltpu.VMEM((n, H, nb * TB), jnp.float32),
            dma((5,)), dma((1,)), dma((C - 1, 2 * half)), dma((4,)), dma((1,)), dma((1,)),
        ],
        compiler_params=pltpu.CompilerParams(
            collective_id=0, has_side_effects=True, vmem_limit_bytes=VMEM_LIMIT
        ),
    )(*given)
    return pl.pallas_call(
        finish,
        out_shape=(
            jax.ShapeDtypeStruct((H, nb, TB), jnp.float32),
            jax.ShapeDtypeStruct(gate_query.shape, jnp.float32),
            jax.ShapeDtypeStruct(gate_key.shape, jnp.float32),
        ),
        in_specs=[vm] * 6,
        out_specs=(hbm,) * 3,
        scratch_shapes=[
            pltpu.VMEM(gate_query.shape, jnp.float32),
            pltpu.VMEM(gate_key.shape, jnp.float32),
            dma((3,)),
        ],
        compiler_params=pltpu.CompilerParams(vmem_limit_bytes=VMEM_LIMIT),
    )(*parts)


def solution(mesh):
    R, C = mesh.shape["row"], mesh.shape["ctx"]
    in_specs = (P(None, ("row", "ctx"), None), P("ctx", None), P(), P(), P())
    out_specs = (P(None, ("row", "ctx"), None), P(), P())
    return jax.shard_map(
        functools.partial(shards, R, C), mesh=mesh, in_specs=in_specs, out_specs=out_specs,
        check_vma=False,
    )
```
